128 devices in a mesh: seq: 32 (over y, z, core), head: 4 (over x).
Axes of the slice: x: 4, y: 4, z: 4, core: 2. Of those that a mesh axis runs over, the one named last changes fastest.
Arguments:
- queries: bfloat16 [131072, 2048], P('seq', 'head'), may hold values from -6 to 6
- keys: bfloat16 [131072, 2048], P('seq', 'head'), may hold values from -0.59765625 to 0.59765625
- values: bfloat16 [131072, 2048], P('seq', 'head'), may hold values from -6 to 6
- norm_gain: float32 [2048], replicated, may hold values from 0.1 to 1.9
Outputs:
- normed: bfloat16 [131072, 2048], P(('seq', 'head'))
The draws below stay inside these ranges and needn't reach their ends.
All inputs are finite; a program needn't handle non-finite values.
Results may differ from the reference program's by a relative error of at most 0.0058.
Values may be sent and summed in bfloat16 or wider, within the bound.
A program may use at most 128 MiB of HBM per device.

```python
import jax
import jax.numpy as jnp
from jax import lax

DH = 128
H = 16
BLK = 512
TOKENS = 131072
F = 2048


def steps_of(stream_key, dims, split, smallest, largest):
    def one(dim, shards_of):
        steps = jax.random.uniform(jax.random.fold_in(jax.random.fold_in(stream_key, 6), dim), (shards_of,), jnp.float32, smallest / len(split), largest / len(split))
        return jnp.repeat(jnp.exp(steps), dims[dim] // shards_of).reshape((-1,) + (1,) * (len(dims) - dim - 1))

    gain = one(*split[0])
    for cut in split[1:]:
        gain = gain * one(*cut)
    return gain


def noise(rng, dims, spread, bound, shards=(), kind=jnp.bfloat16):
    entries = jax.random.normal(rng, dims, jnp.float32) * spread
    if len(shards) > 0:
        entries = steps_of(rng, dims, shards, -0.22, 0.18) * entries
    return jnp.clip(entries, min=-bound, max=bound).astype(kind)


def setup_inputs(seed: int = 0) -> dict:
    seeds = jax.random.split(jax.random.key(seed), 5)
    queries = noise(seeds[0], (TOKENS, F), 1.0, 6.0, ((0, 32), (1, 4)))
    keys = noise(seeds[1], (TOKENS, F), 0.088, 0.59765625, ((0, 32), (1, 4)))
    values = noise(seeds[2], (TOKENS, F), 1.0, 6.0, ((0, 32), (1, 4)))
    norm_gain = jnp.clip(1.0 + 0.18 * jax.random.normal(seeds[3], (F,), jnp.float32), 0.1, 1.9)
    return {"queries": queries, "keys": keys, "values": values, "norm_gain": norm_gain}


def reference(queries, keys, values, norm_gain):
    blocks = TOKENS // BLK

    def split_heads(array):
        return array.reshape(blocks, BLK, H, DH).transpose(2, 0, 1, 3)

    def one_head(operands):
        query_rows, key_rows, value_rows = operands
        query_rows = query_rows.astype(jnp.float32)
        key_rows = key_rows.astype(jnp.float32)
        value_rows = value_rows.astype(jnp.float32)
        block_state = jnp.einsum('nbd,nbe->nde', key_rows, value_rows, precision=lax.Precision.HIGHEST)
        running = jnp.cumsum(block_state, axis=0)
        prefix = jnp.concatenate([jnp.zeros((1, DH, DH), jnp.float32), running[:-1]], axis=0)
        prefix_low = prefix.astype(jnp.bfloat16).astype(jnp.float32)
        inter = jnp.einsum('nbd,nde->nbe', query_rows, prefix_low, precision=lax.Precision.HIGHEST)
        scores = jnp.einsum('nbd,ncd->nbc', query_rows, key_rows, precision=lax.Precision.HIGHEST)
        causal = jnp.arange(BLK)[:, None] >= jnp.arange(BLK)[None, :]
        scores = jnp.where(causal[None], scores, jnp.zeros_like(scores))
        scores = scores.astype(jnp.bfloat16).astype(jnp.float32)
        intra = jnp.einsum('nbc,nce->nbe', scores, value_rows, precision=lax.Precision.HIGHEST)
        return (inter + intra).astype(jnp.bfloat16)
    attention = lax.map(one_head, (split_heads(queries), split_heads(keys), split_heads(values)))
    attention = attention.transpose(1, 2, 0, 3).reshape(TOKENS, F)
    widened = attention.astype(jnp.float32)
    meansq = lax.optimization_barrier(jnp.mean(widened * widened, axis=-1, keepdims=True))
    return (widened * lax.rsqrt(meansq + 1e-06) * norm_gain[None, :]).astype(jnp.bfloat16)
```

```python
import jax
import jax.numpy as jnp
from jax import lax
from jax.experimental import pallas as pl
from jax.experimental.pallas import tpu as pltpu
from jax.sharding import PartitionSpec as P

DH = 128
BLK = 512
HALF = BLK // 2
MESH = pl.DeviceIdType.MESH
F32 = jnp.float32
BF16 = jnp.bfloat16


def dot(a, b, dims):
    return lax.dot_general(a, b, (dims, ((), ())), preferred_element_type=F32)


def make_kernel(seqs, groups, rows, width):
    heads = width // DH
    blocks = rows // BLK
    own = rows // groups
    part = (heads * DH) // seqs
    per = own // BLK
    pieces = own // HALF
    sending = (groups - 1) * per

    def kernel(q_hbm, k_hbm, v_hbm, g_ref, o_hbm, q, k, v, st, tot, got, pre, before, acc, att, rcv,
               in_sem, out_sem, scan_send, scan_recv, send_sem, recv_sem):
        me = lax.axis_index("head")
        my = lax.axis_index("seq")

        def load(i, n):
            hbm, ref = ((k_hbm, k), (v_hbm, v), (q_hbm, q))[i]
            sl = pl.ds(pl.multiple_of(n * BLK, BLK), BLK)
            return pltpu.make_async_copy(hbm.at[sl], ref.at[sl], in_sem.at[i, n])

        for n in range(blocks):
            load(0, n).start()
            load(1, n).start()
        for n in range(blocks):
            load(2, n).start()

        barrier = pltpu.get_barrier_semaphore()

        @pl.loop(1, seqs)
        def _(i):
            pl.semaphore_signal(barrier, inc=1, device_id={"seq": lax.rem(my + i, seqs)}, device_id_type=MESH)

        for d in range(1, groups):
            pl.semaphore_signal(barrier, inc=1, device_id={"head": lax.rem(me + d, groups)}, device_id_type=MESH)

        tot[...] = jnp.zeros_like(tot)

        @pl.loop(0, blocks)
        def _(n):
            load(0, n).wait()
            load(1, n).wait()
            sl = pl.ds(pl.multiple_of(n * BLK, BLK), BLK)
            for h in range(heads):
                hs = slice(h * DH, (h + 1) * DH)
                state = dot(k[sl, hs], v[sl, hs], ((0,), (0,)))
                run = tot[hs, :]
                st[n, hs, :] = run
                tot[hs, :] = run + state

        pl.semaphore_wait(barrier, seqs - 1 + groups - 1)

        def mine(i):
            return pl.ds(pl.multiple_of(i * part, part), part)

        def first(i):
            return pltpu.make_async_remote_copy(
                src_ref=tot.at[mine(i)], dst_ref=got.at[my], send_sem=scan_send.at[0], recv_sem=scan_recv.at[0],
                device_id={"seq": i}, device_id_type=MESH)

        def second(i):
            return pltpu.make_async_remote_copy(
                src_ref=pre.at[i], dst_ref=before.at[mine(my)], send_sem=scan_send.at[1], recv_sem=scan_recv.at[1],
                device_id={"seq": i}, device_id_type=MESH)

        def all_of(stage):
            ref = got.at[pl.ds(0, seqs - 1)]
            return pltpu.make_async_remote_copy(
                src_ref=ref, dst_ref=ref, send_sem=scan_send.at[stage], recv_sem=scan_recv.at[stage],
                device_id={"seq": lax.rem(my + 1, seqs)}, device_id_type=MESH)

        @pl.loop(1, seqs)
        def _(i):
            first(lax.rem(my + i, seqs)).start()

        got[my] = tot[mine(my), :]

        row = lax.broadcasted_iota(jnp.int32, (HALF, HALF), 0)
        col = lax.broadcasted_iota(jnp.int32, (HALF, HALF), 1)
        causal = row >= col

        def step_of(j):
            i = lax.rem(j, groups - 1)
            d = jnp.where(j < sending, 1 + lax.rem(2 * i, groups - 1), 0)
            piece = jnp.where(j < sending, j // (groups - 1), j - sending)
            dest = lax.rem(me + d, groups)
            return d, piece, dest, dest * per + piece

        def local(j):
            _, _, _, n = step_of(j)
            lo = pl.ds(pl.multiple_of(n * BLK, BLK), HALF)
            hi = pl.ds(pl.multiple_of(n * BLK + HALF, HALF), HALF)
            for h in range(heads):
                hs = slice(h * DH, (h + 1) * DH)
                k_lo, k_hi, v_lo, v_hi = k[lo, hs], k[hi, hs], v[lo, hs], v[hi, hs]
                q_lo, q_hi = q[lo, hs], q[hi, hs]
                s = jnp.where(causal, dot(q_lo, k_lo, ((1,), (1,))), 0.0).astype(BF16)
                acc[lo, hs] = dot(s, v_lo, ((1,), (0,)))
                s_l = dot(q_hi, k_lo, ((1,), (1,))).astype(BF16)
                s_h = jnp.where(causal, dot(q_hi, k_hi, ((1,), (1,))), 0.0).astype(BF16)
                acc[hi, hs] = dot(s_l, v_lo, ((1,), (0,))) + dot(s_h, v_hi, ((1,), (0,)))

        for n in range(blocks):
            load(2, n).wait()

        @pl.loop(0, sending // 2)
        def _(j):
            local(j)

        all_of(0).wait_recv()
        run = jnp.zeros((part, DH), F32)
        for i in range(seqs):
            pre[i] = run
            run = run + got[i]

        @pl.loop(1, seqs)
        def _(i):
            second(lax.rem(my + i, seqs)).start()

        before[mine(my), :] = pre[my]

        @pl.loop(sending // 2, sending)
        def _(j):
            local(j)

        all_of(1).wait_recv()

        def exchange(d, n, half):
            dest = lax.rem(me + d, groups)
            to = pl.ds(pl.multiple_of((n - dest * per) * BLK + half * HALF, HALF), HALF)
            at = pl.ds(pl.multiple_of(n * BLK + half * HALF, HALF), HALF)
            piece = (n - dest * per) * 2 + half
            return pltpu.make_async_remote_copy(
                src_ref=att.at[at], dst_ref=rcv.at[to, pl.ds(pl.multiple_of(me * width, width), width)],
                send_sem=send_sem.at[d, piece], recv_sem=recv_sem.at[d, piece],
                device_id={"head": dest}, device_id_type=MESH)

        def arrival(d, piece):
            src = lax.rem(me + groups - d, groups)
            at = pl.ds(pl.multiple_of(piece * HALF, HALF), HALF)
            return pltpu.make_async_remote_copy(
                src_ref=att.at[at], dst_ref=rcv.at[at, pl.ds(pl.multiple_of(src * width, width), width)],
                send_sem=send_sem.at[d, piece], recv_sem=recv_sem.at[d, piece],
                device_id={"head": src}, device_id_type=MESH)

        def rows_of(n, half, h):
            at = pl.ds(pl.multiple_of(n * BLK + half * HALF, HALF), HALF)
            hs = slice(h * DH, (h + 1) * DH)
            low = (before[hs, :] + st[n, hs, :]).astype(BF16)
            return (acc[at, hs] + dot(q[at, hs], low, ((1,), (0,)))).astype(BF16)

        @pl.loop(0, sending)
        def _(j):
            d, _, _, n = step_of(j)
            for half in range(2):
                at = pl.ds(pl.multiple_of(n * BLK + half * HALF, HALF), HALF)
                for h in range(heads):
                    att[at, h * DH:(h + 1) * DH] = rows_of(n, half, h)
                exchange(d, n, half).start()

        @pl.loop(sending, blocks)
        def _(j):
            _, piece, _, n = step_of(j)
            local(j)
            for half in range(2):
                to = pl.ds(pl.multiple_of(piece * BLK + half * HALF, HALF), HALF)
                for h in range(heads):
                    rcv[to, pl.ds(pl.multiple_of(me * width + h * DH, DH), DH)] = rows_of(n, half, h)

        def store(piece):
            at = pl.ds(pl.multiple_of(piece * HALF, HALF), HALF)
            return pltpu.make_async_copy(rcv.at[at], o_hbm.at[at], out_sem.at[piece])

        @pl.loop(0, pieces)
        def _(piece):
            for d in range(1, groups):
                arrival(d, piece).wait_recv()

            @pl.loop(0, HALF // 32)
            def _(i):
                at = pl.ds(pl.multiple_of(piece * HALF + i * 32, 32), 32)
                wide = rcv[at, :].astype(F32)
                mean = jnp.mean(wide * wide, axis=-1, keepdims=True)
                rcv[at, :] = (wide * lax.rsqrt(mean + 1e-06) * g_ref[...]).astype(BF16)

            store(piece).start()

        @pl.loop(0, pieces)
        def _(piece):
            store(piece).wait()
            for d in range(1, groups):
                arrival(d, piece).wait_send()

        all_of(0).wait_send()
        all_of(1).wait_send()

    return kernel


def solution(mesh):
    seqs, groups = mesh.shape["seq"], mesh.shape["head"]

    def shards(queries, keys, values, norm_gain):
        rows, width = queries.shape
        heads = width // DH
        blocks = rows // BLK
        own = rows // groups
        full = width * groups
        part = width // seqs
        any_spec = pl.BlockSpec(memory_space=pl.ANY)
        return pl.pallas_call(
            make_kernel(seqs, groups, rows, width),
            out_shape=jax.ShapeDtypeStruct((own, full), BF16),
            in_specs=[any_spec] * 3 + [pl.BlockSpec(memory_space=pltpu.VMEM)],
            out_specs=any_spec,
            scratch_shapes=[
                pltpu.VMEM((rows, width), BF16),
                pltpu.VMEM((rows, width), BF16),
                pltpu.VMEM((rows, width), BF16),
                pltpu.VMEM((blocks, width, DH), F32),
                pltpu.VMEM((width, DH), F32),
                pltpu.VMEM((seqs, part, DH), F32),
                pltpu.VMEM((seqs, part, DH), F32),
                pltpu.VMEM((width, DH), F32),
                pltpu.VMEM((rows, width), F32),
                pltpu.VMEM((rows, width), BF16),
                pltpu.VMEM((own, full), BF16),
                pltpu.SemaphoreType.DMA((3, blocks)),
                pltpu.SemaphoreType.DMA((own // HALF,)),
                pltpu.SemaphoreType.DMA((2,)),
                pltpu.SemaphoreType.DMA((2,)),
                pltpu.SemaphoreType.DMA((groups, own // HALF)),
                pltpu.SemaphoreType.DMA((groups, own // HALF)),
            ],
            compiler_params=pltpu.CompilerParams(
                collective_id=0, has_side_effects=True, vmem_limit_bytes=56 << 20),
            name="attention_norm",
        )(queries, keys, values, norm_gain[None, :])

    return jax.shard_map(
        shards,
        mesh=mesh,
        in_specs=(P("seq", "head"), P("seq", "head"), P("seq", "head"), P()),
        out_specs=P(("seq", "head"), None),
        check_vma=False,
    )
```

```python
import jax
import jax.numpy as jnp
from jax import lax
from jax.experimental import pallas as pl
from jax.experimental.pallas import tpu as pltpu
from jax.sharding import PartitionSpec as P

DH = 128
BLK = 512
HALF = BLK // 2
MESH = pl.DeviceIdType.MESH
F32 = jnp.float32
BF16 = jnp.bfloat16


def dot(a, b, dims):
    return lax.dot_general(a, b, (dims, ((), ())), preferred_element_type=F32)


def offsets(seqs):
    side = 1
    while side * side * 2 < seqs:
        side += 1
    assert side * side * 2 == seqs

    def hops(step):
        return min(step, side - step)

    steps = [(y, z, c) for y in range(side) for z in range(side) for c in range(2)]
    steps.remove((0, 0, 0))
    return side, sorted(steps, key=lambda s: (-hops(s[0]) - hops(s[1]), s))


def make_kernel(seqs, groups, rows, width):
    assert groups == 4
    heads = width // DH
    blocks = rows // BLK
    own = rows // groups
    part = (heads * DH) // seqs
    per = own // BLK
    pieces = own // HALF
    side, steps = offsets(seqs)
    later = tuple(range(1, heads))
    every = tuple(range(heads))

    def kernel(q_hbm, k_hbm, v_hbm, g_hbm, out, q, k, v, gain, st, tot, got, pre, before, acc, att, rcv,
               q_out, q_in, l_out, l_in, p_out, p_in,
               in_sem, gain_sem, scan_send, scan_recv, send_sem, recv_sem, q_sems, l_sems, p_sems):
        me = lax.axis_index("head")
        my = lax.axis_index("seq")

        def block(n):
            return pl.ds(pl.multiple_of(n * BLK, BLK), BLK)

        def half_of(n, half):
            return pl.ds(pl.multiple_of(n * BLK + half * HALF, HALF), HALF)

        def load(i, n):
            hbm, ref = ((k_hbm, k), (v_hbm, v), (q_hbm, q))[i]
            return pltpu.make_async_copy(hbm.at[block(n)], ref.at[block(n)], in_sem.at[i, n])

        for n in range(blocks):
            load(0, n).start()
            load(1, n).start()
        for n in range(blocks):
            load(2, n).start()
        load_gain = pltpu.make_async_copy(g_hbm, gain, gain_sem)
        load_gain.start()

        barrier = pltpu.get_barrier_semaphore()

        @pl.loop(1, seqs)
        def _(i):
            pl.semaphore_signal(barrier, inc=1, device_id={"seq": lax.rem(my + i, seqs)}, device_id_type=MESH)

        for d in range(1, groups):
            pl.semaphore_signal(barrier, inc=1, device_id={"head": lax.rem(me + d, groups)}, device_id_type=MESH)

        tot[...] = jnp.zeros_like(tot)

        @pl.loop(0, blocks)
        def _(n):
            load(0, n).wait()
            load(1, n).wait()
            for h in range(heads):
                hs = slice(h * DH, (h + 1) * DH)
                state = dot(k[block(n), hs], v[block(n), hs], ((0,), (0,)))
                run = tot[hs, :]
                st[n, hs, :] = run
                tot[hs, :] = run + state

        for n in range(blocks):
            load(2, n).wait()

        def first_block(d):
            return lax.rem(me + d, groups) * per

        for slot in range(2):
            at = pl.ds(pl.multiple_of(first_block(1 + 2 * slot) * BLK, BLK), own)
            q_out[slot] = q[at, :DH]

        pl.semaphore_wait(barrier, seqs - 1 + groups - 1)

        def mine(i):
            return pl.ds(pl.multiple_of(i * part, part), part)

        def first(i):
            return pltpu.make_async_remote_copy(
                src_ref=tot.at[mine(i)], dst_ref=got.at[my], send_sem=scan_send.at[0], recv_sem=scan_recv.at[0],
                device_id={"seq": i}, device_id_type=MESH)

        def second(i):
            return pltpu.make_async_remote_copy(
                src_ref=pre.at[i], dst_ref=before.at[my], send_sem=scan_send.at[1], recv_sem=scan_recv.at[1],
                device_id={"seq": i}, device_id_type=MESH)

        def all_of(stage):
            ref = (got, before)[stage].at[pl.ds(0, seqs - 1)]
            return pltpu.make_async_remote_copy(
                src_ref=ref, dst_ref=ref, send_sem=scan_send.at[stage], recv_sem=scan_recv.at[stage],
                device_id={"seq": lax.rem(my + 1, seqs)}, device_id_type=MESH)

        my_y, my_z, my_c = my // (2 * side), lax.rem(my // 2, side), lax.rem(my, 2)

        def away(step):
            y = lax.rem(my_y + step[0], side)
            z = lax.rem(my_z + step[1], side)
            return (y * side + z) * 2 + lax.rem(my_c + step[2], 2)

        for step in steps:
            first(away(step)).start()

        def ahead(src, dst, sems, slot, *which):
            return pltpu.make_async_remote_copy(
                src_ref=src, dst_ref=dst, send_sem=sems.at[(0, slot) + which], recv_sem=sems.at[(1, slot) + which],
                device_id={"head": lax.rem(me + 1 + 2 * slot, groups)}, device_id_type=MESH)

        def send_q(slot):
            return ahead(q_out.at[slot], q_in.at[slot], q_sems, slot)

        def send_l(slot, piece):
            return ahead(l_out.at[slot, block(piece)], l_in.at[slot, block(piece)], l_sems, slot, piece)

        def send_p(slot):
            return ahead(p_out, p_in.at[slot], p_sems, slot)

        for slot in range(2):
            send_q(slot).start()

        got[my] = tot[mine(my), :]

        row = lax.broadcasted_iota(jnp.int32, (HALF, HALF), 0)
        col = lax.broadcasted_iota(jnp.int32, (HALF, HALF), 1)
        causal = row >= col

        def local(n, h):
            hs = slice(h * DH, (h + 1) * DH)
            lo, hi = half_of(n, 0), half_of(n, 1)
            k_lo, k_hi, v_lo, v_hi = k[lo, hs], k[hi, hs], v[lo, hs], v[hi, hs]
            q_lo, q_hi = q[lo, hs], q[hi, hs]
            s = jnp.where(causal, dot(q_lo, k_lo, ((1,), (1,))), 0.0).astype(BF16)
            s_l = dot(q_hi, k_lo, ((1,), (1,))).astype(BF16)
            s_h = jnp.where(causal, dot(q_hi, k_hi, ((1,), (1,))), 0.0).astype(BF16)
            return (dot(s, v_lo, ((1,), (0,))),
                    dot(s_l, v_lo, ((1,), (0,))) + dot(s_h, v_hi, ((1,), (0,))))

        @pl.loop(0, 2 * per)
        def _(e):
            slot, piece = lax.rem(e, 2), e // 2
            n = first_block(1 + 2 * slot) + piece
            low = st[n, :DH, :].astype(BF16)
            for half, value in enumerate(local(n, 0)):
                value = value + dot(q[half_of(n, half), :DH], low, ((1,), (0,)))
                l_out[slot, half_of(piece, half), :] = value.astype(BF16)
            send_l(slot, piece).start()

        def keep(n, which):
            for h in which:
                hs = slice(h * DH, (h + 1) * DH)
                acc[half_of(n, 0), hs], acc[half_of(n, 1), hs] = local(n, h)

        def keep_sides(piece):
            @pl.loop(0, 2)
            def _(slot):
                keep(first_block(1 + 2 * slot) + piece, later)

        keep_sides(0)

        all_of(0).wait_recv()
        run = jnp.zeros((part, DH), F32)
        for i in range(seqs):
            pre[i] = run.astype(BF16)
            run = run + got[i]

        for step in steps:
            second(away(step)).start()

        before[my] = pre[my]

        keep(first_block(2), every)

        all_of(1).wait_recv()

        def state(n, h):
            some = slice(h * DH // part, (h + 1) * DH // part)
            old = before[some].reshape(DH, DH).astype(F32)
            return old + st[n, h * DH:(h + 1) * DH, :]

        p_out[...] = before[:DH // part].reshape(DH, DH)
        for slot in range(2):
            send_p(slot).start()

        def exchange(d, piece, half, skip, source):
            partner = lax.rem(me + (groups - d if source else d), groups)
            owner = partner if source else me
            to = half_of(piece, half)
            at = to if source else half_of(partner * per + piece, half)
            cols = pl.ds(pl.multiple_of(owner * width + skip * DH, DH), width - skip * DH)
            which = (d, piece * 2 + half)
            return pltpu.make_async_remote_copy(
                src_ref=att.at[at, pl.ds(skip * DH, width - skip * DH)], dst_ref=rcv.at[to, cols],
                send_sem=send_sem.at[which], recv_sem=recv_sem.at[which],
                device_id={"head": partner}, device_id_type=MESH)

        def rows_of(n, half, h):
            hs = slice(h * DH, (h + 1) * DH)
            at = half_of(n, half)
            low = state(n, h).astype(BF16)
            return (acc[at, hs] + dot(q[at, hs], low, ((1,), (0,)))).astype(BF16)

        def finish(d, piece, which):
            n = first_block(d) + piece
            for half in range(2):
                for h in which:
                    att[half_of(n, half), h * DH:(h + 1) * DH] = rows_of(n, half, h)
                exchange(d, piece, half, which[0], False).start()

        def finish_sides(piece):
            @pl.loop(0, 2)
            def _(slot):
                finish(1 + 2 * slot, piece, later)

        finish_sides(0)
        finish(2, 0, every)

        @pl.loop(1, per)
        def _(piece):
            keep_sides(piece)
            finish_sides(piece)
            keep(first_block(2) + piece, every)
            finish(2, piece, every)

        @pl.loop(0, per)
        def _(piece):
            n = me * per + piece
            keep(n, every)
            for half in range(2):
                for h in every:
                    cols = pl.ds(pl.multiple_of(me * width + h * DH, DH), DH)
                    rcv[half_of(piece, half), cols] = rows_of(n, half, h)

        for slot in range(2):
            send_q(slot).wait_recv()
            send_p(slot).wait_recv()

        @pl.loop(0, per)
        def _(piece):
            for slot in range(2):
                send_l(slot, piece).wait_recv()
                src = lax.rem(me + groups - 1 - 2 * slot, groups)
                cols = pl.ds(pl.multiple_of(src * width, DH), DH)
                for half in range(2):
                    at = half_of(piece, half)
                    value = dot(q_in[slot, at, :], p_in[slot], ((1,), (0,)))
                    rcv[at, cols] = (l_in[slot, at, :].astype(F32) + value).astype(BF16)

        load_gain.wait()

        @pl.loop(0, pieces)
        def _(i):
            piece, half = i // 2, lax.rem(i, 2)
            for d, skip in ((1, 1), (3, 1), (2, 0)):
                exchange(d, piece, half, skip, True).wait_recv()

            @pl.loop(0, HALF // 32)
            def _(j):
                at = pl.ds(pl.multiple_of(i * HALF + j * 32, 32), 32)
                wide = rcv[at, :].astype(F32)
                mean = jnp.mean(wide * wide, axis=-1, keepdims=True)
                out[at, :] = (wide * lax.rsqrt(mean + 1e-06) * gain[...]).astype(BF16)

        @pl.loop(0, pieces)
        def _(i):
            for d, skip in ((1, 1), (3, 1), (2, 0)):
                exchange(d, i // 2, lax.rem(i, 2), skip, False).wait_send()

        for slot in range(2):
            send_q(slot).wait_send()
            send_p(slot).wait_send()
            for piece in range(per):
                send_l(slot, piece).wait_send()

        all_of(0).wait_send()
        all_of(1).wait_send()

    return kernel


def solution(mesh):
    seqs, groups = mesh.shape["seq"], mesh.shape["head"]

    def shards(queries, keys, values, norm_gain):
        rows, width = queries.shape
        blocks = rows // BLK
        own = rows // groups
        per = own // BLK
        full = width * groups
        part = width // seqs
        dma = pltpu.SemaphoreType.DMA
        return pl.pallas_call(
            make_kernel(seqs, groups, rows, width),
            out_shape=pltpu.VMEM((own, full), BF16),
            in_specs=[pl.BlockSpec(memory_space=pl.ANY)] * 4,
            out_specs=pl.BlockSpec(memory_space=pltpu.VMEM),
            scratch_shapes=[
                pltpu.VMEM((rows, width), BF16),
                pltpu.VMEM((rows, width), BF16),
                pltpu.VMEM((rows, width), BF16),
                pltpu.VMEM((1, full), F32),
                pltpu.VMEM((blocks, width, DH), F32),
                pltpu.VMEM((width, DH), F32),
                pltpu.VMEM((seqs, part, DH), F32),
                pltpu.VMEM((seqs, part, DH), BF16),
                pltpu.VMEM((seqs, part, DH), BF16),
                pltpu.VMEM((rows, width), F32),
                pltpu.VMEM((rows, width), BF16),
                pltpu.VMEM((own, full), BF16),
                pltpu.VMEM((2, own, DH), BF16),
                pltpu.VMEM((2, own, DH), BF16),
                pltpu.VMEM((2, own, DH), BF16),
                pltpu.VMEM((2, own, DH), BF16),
                pltpu.VMEM((DH, DH), BF16),
                pltpu.VMEM((2, DH, DH), BF16),
                dma((3, blocks)),
                dma,
                dma((2,)),
                dma((2,)),
                dma((groups, own // HALF)),
                dma((groups, own // HALF)),
                dma((2, 2)),
                dma((2, 2, per)),
                dma((2, 2)),
            ],
            compiler_params=pltpu.CompilerParams(
                collective_id=0, has_side_effects=True, vmem_limit_bytes=48 << 20),
            name="attention_norm",
        )(queries, keys, values, norm_gain[None, :])

    return jax.shard_map(
        shards,
        mesh=mesh,
        in_specs=(P("seq", "head"), P("seq", "head"), P("seq", "head"), P()),
        out_specs=P(("seq", "head"), None),
        check_vma=False,
    )
```

```python
import jax
import jax.numpy as jnp
from jax import lax
from jax.experimental import pallas as pl
from jax.experimental.pallas import tpu as pltpu
from jax.sharding import PartitionSpec as P

DH = 128
BLK = 512
HALF = BLK // 2
PIECE = 128
MESH = pl.DeviceIdType.MESH
F32 = jnp.float32
BF16 = jnp.bfloat16


def dot(a, b, dims):
    return lax.dot_general(a, b, (dims, ((), ())), preferred_element_type=F32)


def offsets(seqs):
    side = 1
    while side * side * 2 < seqs:
        side += 1
    assert side * side * 2 == seqs

    def hops(step):
        return min(step, side - step)

    steps = [(y, z, c) for y in range(side) for z in range(side) for c in range(2)]
    steps.remove((0, 0, 0))
    return side, sorted(steps, key=lambda s: (-hops(s[0]) - hops(s[1]), s))


def make_kernel(seqs, groups, rows, width):
    assert groups == 4
    heads = width // DH
    blocks = rows // BLK
    own = rows // groups
    part = (heads * DH) // seqs
    per = own // BLK
    pieces = own // PIECE
    cuts = HALF // PIECE
    side, steps = offsets(seqs)
    later = tuple(range(1, heads))
    every = tuple(range(heads))

    def kernel(q_hbm, k_hbm, v_hbm, g_hbm, out, q, k, v, gain, st, tot, got, pre, before, acc, att, rcv,
               q_in, l_out, l_in, p_out, p_in,
               in_sem, gain_sem, scan_send, scan_recv, send_sem, recv_sem, q_sems, l_sems, p_sems):
        me = lax.axis_index("head")
        my = lax.axis_index("seq")

        def block(n):
            return pl.ds(pl.multiple_of(n * BLK, BLK), BLK)

        def half_of(n, half):
            return pl.ds(pl.multiple_of(n * BLK + half * HALF, HALF), HALF)

        def load(i, n):
            hbm, ref = ((k_hbm, k), (v_hbm, v), (q_hbm, q))[i]
            return pltpu.make_async_copy(hbm.at[block(n)], ref.at[block(n)], in_sem.at[i, n])

        for n in range(blocks):
            load(0, n).start()
            load(1, n).start()
        load_gain = pltpu.make_async_copy(g_hbm, gain, gain_sem)
        load_gain.start()

        my_y, my_z, my_c = my // (2 * side), lax.rem(my // 2, side), lax.rem(my, 2)

        def away(step):
            y = lax.rem(my_y + step[0], side)
            z = lax.rem(my_z + step[1], side)
            return (y * side + z) * 2 + lax.rem(my_c + step[2], 2)

        def first_block(d):
            return lax.rem(me + d, groups) * per

        barrier = pltpu.get_barrier_semaphore()
        for d in range(1, groups):
            pl.semaphore_signal(barrier, inc=1, device_id={"head": lax.rem(me + d, groups)}, device_id_type=MESH)
        for step in steps:
            pl.semaphore_signal(barrier, inc=1, device_id={"seq": away(step)}, device_id_type=MESH)

        def ahead(src, dst, sems, slot, *which):
            return pltpu.make_async_remote_copy(
                src_ref=src, dst_ref=dst, send_sem=sems.at[(0, slot) + which], recv_sem=sems.at[(1, slot) + which],
                device_id={"head": lax.rem(me + 1 + 2 * slot, groups)}, device_id_type=MESH)

        def send_q(slot):
            at = pl.ds(pl.multiple_of(first_block(1 + 2 * slot) * BLK, BLK), own)
            return ahead(q_hbm.at[at, pl.ds(0, DH)], q_in.at[slot], q_sems, slot)

        def send_l(slot, piece):
            return ahead(l_out.at[slot, block(piece)], l_in.at[slot, block(piece)], l_sems, slot, piece)

        def send_p(slot):
            return ahead(p_out, p_in.at[slot], p_sems, slot)

        tot[...] = jnp.zeros_like(tot)

        def gather(n):
            load(0, n).wait()
            load(1, n).wait()
            for h in range(heads):
                hs = slice(h * DH, (h + 1) * DH)
                state = dot(k[block(n), hs], v[block(n), hs], ((0,), (0,)))
                run = tot[hs, :]
                st[n, hs, :] = run
                tot[hs, :] = run + state

        pl.loop(0, 7)(gather)

        pl.semaphore_wait(barrier, seqs - 1 + groups - 1)

        for slot in range(2):
            send_q(slot).start()

        pl.loop(7, blocks)(gather)

        def mine(i):
            return pl.ds(pl.multiple_of(i * part, part), part)

        def first(i):
            return pltpu.make_async_remote_copy(
                src_ref=tot.at[mine(i)], dst_ref=got.at[my], send_sem=scan_send.at[0], recv_sem=scan_recv.at[0],
                device_id={"seq": i}, device_id_type=MESH)

        def second(i):
            return pltpu.make_async_remote_copy(
                src_ref=pre.at[i], dst_ref=before.at[my], send_sem=scan_send.at[1], recv_sem=scan_recv.at[1],
                device_id={"seq": i}, device_id_type=MESH)

        def all_of(stage):
            ref = (got, before)[stage].at[pl.ds(0, seqs - 1)]
            return pltpu.make_async_remote_copy(
                src_ref=ref, dst_ref=ref, send_sem=scan_send.at[stage], recv_sem=scan_recv.at[stage],
                device_id={"seq": lax.rem(my + 1, seqs)}, device_id_type=MESH)

        for n in range(blocks):
            load(2, n).start()

        for step in steps:
            first(away(step)).start()

        got[my] = tot[mine(my), :]

        row = lax.broadcasted_iota(jnp.int32, (HALF, HALF), 0)
        col = lax.broadcasted_iota(jnp.int32, (HALF, HALF), 1)
        causal = row >= col

        def local(n, h):
            hs = slice(h * DH, (h + 1) * DH)
            lo, hi = half_of(n, 0), half_of(n, 1)
            k_lo, k_hi, v_lo, v_hi = k[lo, hs], k[hi, hs], v[lo, hs], v[hi, hs]
            q_lo, q_hi = q[lo, hs], q[hi, hs]
            s = jnp.where(causal, dot(q_lo, k_lo, ((1,), (1,))), 0.0).astype(BF16)
            s_l = dot(q_hi, k_lo, ((1,), (1,))).astype(BF16)
            s_h = jnp.where(causal, dot(q_hi, k_hi, ((1,), (1,))), 0.0).astype(BF16)
            return (dot(s, v_lo, ((1,), (0,))),
                    dot(s_l, v_lo, ((1,), (0,))) + dot(s_h, v_hi, ((1,), (0,))))

        for n in range(blocks):
            load(2, n).wait()

        @pl.loop(0, 2 * per)
        def _(e):
            slot, piece = lax.rem(e, 2), e // 2
            n = first_block(1 + 2 * slot) + piece
            low = st[n, :DH, :].astype(BF16)
            for half, value in enumerate(local(n, 0)):
                value = value + dot(q[half_of(n, half), :DH], low, ((1,), (0,)))
                l_out[slot, half_of(piece, half), :] = value.astype(BF16)
            send_l(slot, piece).start()

        def keep(n, which):
            for h in which:
                hs = slice(h * DH, (h + 1) * DH)
                acc[half_of(n, 0), hs], acc[half_of(n, 1), hs] = local(n, h)

        def keep_sides(piece):
            @pl.loop(0, 2)
            def _(slot):
                keep(first_block(1 + 2 * slot) + piece, later)

        keep_sides(0)

        all_of(0).wait_recv()
        run = jnp.zeros((part, DH), F32)
        for i in range(seqs):
            pre[i] = run.astype(BF16)
            run = run + got[i]

        for step in steps:
            second(away(step)).start()

        before[my] = pre[my]

        keep(first_block(2), every)

        all_of(1).wait_recv()

        def state(n, h):
            some = slice(h * DH // part, (h + 1) * DH // part)
            old = before[some].reshape(DH, DH).astype(F32)
            return old + st[n, h * DH:(h + 1) * DH, :]

        p_out[...] = before[:DH // part].reshape(DH, DH)
        for slot in range(2):
            send_p(slot).start()

        def exchange(d, piece, skip, source):
            partner = lax.rem(me + (groups - d if source else d), groups)
            owner = partner if source else me
            to = pl.ds(pl.multiple_of(piece * PIECE, PIECE), PIECE)
            at = to if source else pl.ds(pl.multiple_of(partner * own + piece * PIECE, PIECE), PIECE)
            cols = pl.ds(pl.multiple_of(owner * width + skip * DH, DH), width - skip * DH)
            return pltpu.make_async_remote_copy(
                src_ref=att.at[at, pl.ds(skip * DH, width - skip * DH)], dst_ref=rcv.at[to, cols],
                send_sem=send_sem.at[d, piece], recv_sem=recv_sem.at[d, piece],
                device_id={"head": partner}, device_id_type=MESH)

        def rows_of(n, half, h):
            hs = slice(h * DH, (h + 1) * DH)
            at = half_of(n, half)
            low = state(n, h).astype(BF16)
            return (acc[at, hs] + dot(q[at, hs], low, ((1,), (0,)))).astype(BF16)

        def finish(d, piece, which):
            n = first_block(d) + piece
            for half in range(2):
                for h in which:
                    att[half_of(n, half), h * DH:(h + 1) * DH] = rows_of(n, half, h)
                for cut in range(cuts):
                    exchange(d, (piece * 2 + half) * cuts + cut, which[0], False).start()

        def finish_sides(piece):
            @pl.loop(0, 2)
            def _(slot):
                finish(1 + 2 * slot, piece, later)

        finish_sides(0)
        finish(2, 0, every)

        @pl.loop(1, per)
        def _(piece):
            keep_sides(piece)
            finish_sides(piece)
            keep(first_block(2) + piece, every)
            finish(2, piece, every)

        @pl.loop(0, per)
        def _(piece):
            n = me * per + piece
            keep(n, every)
            for half in range(2):
                for h in every:
                    cols = pl.ds(pl.multiple_of(me * width + h * DH, DH), DH)
                    rcv[half_of(piece, half), cols] = rows_of(n, half, h)

        for slot in range(2):
            send_q(slot).wait_recv()
            send_p(slot).wait_recv()

        @pl.loop(0, per)
        def _(piece):
            for slot in range(2):
                send_l(slot, piece).wait_recv()
                src = lax.rem(me + groups - 1 - 2 * slot, groups)
                cols = pl.ds(pl.multiple_of(src * width, DH), DH)
                for half in range(2):
                    at = half_of(piece, half)
                    value = dot(q_in[slot, at, :], p_in[slot], ((1,), (0,)))
                    rcv[at, cols] = (l_in[slot, at, :].astype(F32) + value).astype(BF16)

        load_gain.wait()

        @pl.loop(0, pieces)
        def _(i):
            for d, skip in ((1, 1), (3, 1), (2, 0)):
                exchange(d, i, skip, True).wait_recv()

            @pl.loop(0, PIECE // 32)
            def _(j):
                at = pl.ds(pl.multiple_of(i * PIECE + j * 32, 32), 32)
                wide = rcv[at, :].astype(F32)
                mean = jnp.mean(wide * wide, axis=-1, keepdims=True)
                out[at, :] = (wide * lax.rsqrt(mean + 1e-06) * gain[...]).astype(BF16)

        @pl.loop(0, pieces)
        def _(i):
            for d, skip in ((1, 1), (3, 1), (2, 0)):
                exchange(d, i, skip, False).wait_send()

        for slot in range(2):
            send_q(slot).wait_send()
            send_p(slot).wait_send()
            for piece in range(per):
                send_l(slot, piece).wait_send()

        all_of(0).wait_send()
        all_of(1).wait_send()

    return kernel


def solution(mesh):
    seqs, groups = mesh.shape["seq"], mesh.shape["head"]

    def shards(queries, keys, values, norm_gain):
        rows, width = queries.shape
        blocks = rows // BLK
        own = rows // groups
        per = own // BLK
        full = width * groups
        part = width // seqs
        dma = pltpu.SemaphoreType.DMA
        return pl.pallas_call(
            make_kernel(seqs, groups, rows, width),
            out_shape=pltpu.VMEM((own, full), BF16),
            in_specs=[pl.BlockSpec(memory_space=pltpu.HBM)] * 4,
            out_specs=pl.BlockSpec(memory_space=pltpu.VMEM),
            scratch_shapes=[
                pltpu.VMEM((rows, width), BF16),
                pltpu.VMEM((rows, width), BF16),
                pltpu.VMEM((rows, width), BF16),
                pltpu.VMEM((1, full), F32),
                pltpu.VMEM((blocks, width, DH), F32),
                pltpu.VMEM((width, DH), F32),
                pltpu.VMEM((seqs, part, DH), F32),
                pltpu.VMEM((seqs, part, DH), BF16),
                pltpu.VMEM((seqs, part, DH), BF16),
                pltpu.VMEM((rows, width), F32),
                pltpu.VMEM((rows, width), BF16),
                pltpu.VMEM((own, full), BF16),
                pltpu.VMEM((2, own, DH), BF16),
                pltpu.VMEM((2, own, DH), BF16),
                pltpu.VMEM((2, own, DH), BF16),
                pltpu.VMEM((DH, DH), BF16),
                pltpu.VMEM((2, DH, DH), BF16),
                dma((3, blocks)),
                dma,
                dma((2,)),
                dma((2,)),
                dma((groups, own // PIECE)),
                dma((groups, own // PIECE)),
                dma((2, 2)),
                dma((2, 2, per)),
                dma((2, 2)),
            ],
            compiler_params=pltpu.CompilerParams(
                collective_id=0, has_side_effects=True, vmem_limit_bytes=58 << 20),
            name="attention_norm",
        )(queries, keys, values, norm_gain[None, :])

    return jax.shard_map(
        shards,
        mesh=mesh,
        in_specs=(P("seq", "head"), P("seq", "head"), P("seq", "head"), P()),
        out_specs=P(("seq", "head"), None),
        check_vma=False,
    )
```

```python
import jax
import jax.numpy as jnp
from jax import lax
from jax.experimental import pallas as pl
from jax.experimental.pallas import tpu as pltpu
from jax.sharding import PartitionSpec as P

DH = 128
BLK = 512
HALF = BLK // 2
PIECE = 128
MESH = pl.DeviceIdType.MESH
F32 = jnp.float32
BF16 = jnp.bfloat16


def dot(a, b, dims):
    return lax.dot_general(a, b, (dims, ((), ())), preferred_element_type=F32)


def offsets(seqs):
    side = 1
    while side * side * 2 < seqs:
        side += 1
    assert side * side * 2 == seqs

    def hops(step):
        return min(step, side - step)

    steps = [(y, z, c) for y in range(side) for z in range(side) for c in range(2)]
    steps.remove((0, 0, 0))
    return side, sorted(steps, key=lambda s: (-hops(s[0]) - hops(s[1]), s))


def make_kernel(seqs, groups, rows, width):
    assert groups == 4
    heads = width // DH
    blocks = rows // BLK
    own = rows // groups
    part = (heads * DH) // seqs
    per = own // BLK
    pieces = own // PIECE
    cuts = HALF // PIECE
    side, steps = offsets(seqs)
    later = tuple(range(1, heads))
    every = tuple(range(heads))

    def kernel(q_hbm, k_hbm, v_hbm, g_hbm, out, q, k, v, gain, st, tot, got, pre, before, acc, att, rcv,
               q_in, l_out, l_in, p_out, p_in,
               in_sem, gain_sem, scan_send, scan_recv, send_sem, recv_sem, q_sems, l_sems, p_sems):
        me = lax.axis_index("head")
        my = lax.axis_index("seq")

        def block(n):
            return pl.ds(n * BLK if isinstance(n, int) else pl.multiple_of(n * BLK, BLK), BLK)

        def half_of(n, half):
            return pl.ds(pl.multiple_of(n * BLK + half * HALF, HALF), HALF)

        def load(i, n):
            hbm, ref = ((k_hbm, k), (v_hbm, v), (q_hbm, q))[i]
            return pltpu.make_async_copy(hbm.at[block(n)], ref.at[block(n)], in_sem.at[i, n])

        for n in range(blocks):
            load(0, n).start()
            load(1, n).start()
        load_gain = pltpu.make_async_copy(g_hbm, gain, gain_sem)
        load_gain.start()

        my_y, my_z, my_c = my // (2 * side), lax.rem(my // 2, side), lax.rem(my, 2)

        def away(step):
            y = lax.rem(my_y + step[0], side)
            z = lax.rem(my_z + step[1], side)
            return (y * side + z) * 2 + lax.rem(my_c + step[2], 2)

        def first_block(d):
            return lax.rem(me + d, groups) * per

        barrier = pltpu.get_barrier_semaphore()
        for d in range(1, groups):
            pl.semaphore_signal(barrier, inc=1, device_id={"head": lax.rem(me + d, groups)}, device_id_type=MESH)
        for step in steps:
            pl.semaphore_signal(barrier, inc=1, device_id={"seq": away(step)}, device_id_type=MESH)

        def ahead(src, dst, sems, slot, *which):
            return pltpu.make_async_remote_copy(
                src_ref=src, dst_ref=dst, send_sem=sems.at[(0, slot) + which], recv_sem=sems.at[(1, slot) + which],
                device_id={"head": lax.rem(me + 1 + 2 * slot, groups)}, device_id_type=MESH)

        def send_q(slot):
            at = pl.ds(pl.multiple_of(first_block(1 + 2 * slot) * BLK, BLK), own)
            return ahead(q_hbm.at[at, pl.ds(0, DH)], q_in.at[slot], q_sems, slot)

        def send_l(slot, piece):
            return ahead(l_out.at[slot, block(piece)], l_in.at[slot, block(piece)], l_sems, slot, piece)

        def send_p(slot):
            return ahead(p_out, p_in.at[slot], p_sems, slot)

        tot[...] = jnp.zeros_like(tot)

        def gather(start, count):
            for n in range(start, start + count):
                load(0, n).wait()
                load(1, n).wait()
                load(2, n).start()
            for h in range(heads):
                hs = slice(h * DH, (h + 1) * DH)
                run = tot[hs, :]
                for n in range(start, start + count):
                    st[n, hs, :] = run
                    run = run + dot(k[block(n), hs], v[block(n), hs], ((0,), (0,)))
                tot[hs, :] = run

        gather(0, 4)
        gather(4, 2)
        pl.semaphore_wait(barrier, seqs - 1 + groups - 1)
        for slot in range(2):
            send_q(slot).start()
        gather(6, 2)

        def mine(i):
            return pl.ds(pl.multiple_of(i * part, part), part)

        def first(i):
            return pltpu.make_async_remote_copy(
                src_ref=tot.at[mine(i)], dst_ref=got.at[my], send_sem=scan_send.at[0], recv_sem=scan_recv.at[0],
                device_id={"seq": i}, device_id_type=MESH)

        def second(i):
            return pltpu.make_async_remote_copy(
                src_ref=pre.at[i], dst_ref=before.at[my], send_sem=scan_send.at[1], recv_sem=scan_recv.at[1],
                device_id={"seq": i}, device_id_type=MESH)

        def all_of(stage):
            ref = (got, before)[stage].at[pl.ds(0, seqs - 1)]
            return pltpu.make_async_remote_copy(
                src_ref=ref, dst_ref=ref, send_sem=scan_send.at[stage], recv_sem=scan_recv.at[stage],
                device_id={"seq": lax.rem(my + 1, seqs)}, device_id_type=MESH)

        for step in steps:
            first(away(step)).start()

        got[my] = tot[mine(my), :]

        row = lax.broadcasted_iota(jnp.int32, (HALF, HALF), 0)
        col = lax.broadcasted_iota(jnp.int32, (HALF, HALF), 1)
        causal = row >= col

        def local(n, h):
            hs = slice(h * DH, (h + 1) * DH)
            lo, hi = half_of(n, 0), half_of(n, 1)
            k_lo, k_hi, v_lo, v_hi = k[lo, hs], k[hi, hs], v[lo, hs], v[hi, hs]
            q_lo, q_hi = q[lo, hs], q[hi, hs]
            s = jnp.where(causal, dot(q_lo, k_lo, ((1,), (1,))), 0.0).astype(BF16)
            s_l = dot(q_hi, k_lo, ((1,), (1,))).astype(BF16)
            s_h = jnp.where(causal, dot(q_hi, k_hi, ((1,), (1,))), 0.0).astype(BF16)
            return (dot(s, v_lo, ((1,), (0,))),
                    dot(s_l, v_lo, ((1,), (0,))) + dot(s_h, v_hi, ((1,), (0,))))

        for n in range(blocks):
            load(2, n).wait()

        @pl.loop(0, per)
        def _(piece):
            for slot in range(2):
                n = first_block(1 + 2 * slot) + piece
                low = st[n, :DH, :].astype(BF16)
                for half, value in enumerate(local(n, 0)):
                    value = value + dot(q[half_of(n, half), :DH], low, ((1,), (0,)))
                    l_out[slot, half_of(piece, half), :] = value.astype(BF16)
                send_l(slot, piece).start()

        def keep(n, which):
            for h in which:
                hs = slice(h * DH, (h + 1) * DH)
                acc[half_of(n, 0), hs], acc[half_of(n, 1), hs] = local(n, h)

        def keep_sides(piece):
            @pl.loop(0, 2)
            def _(slot):
                keep(first_block(1 + 2 * slot) + piece, later)

        all_of(0).wait_recv()
        run = jnp.zeros((part, DH), F32)
        for i in range(seqs):
            pre[i] = run.astype(BF16)
            run = run + got[i]

        for step in steps:
            second(away(step)).start()

        before[my] = pre[my]

        keep_sides(0)
        keep(first_block(2), every)

        all_of(1).wait_recv()

        def state(n, h):
            some = slice(h * DH // part, (h + 1) * DH // part)
            old = before[some].reshape(DH, DH).astype(F32)
            return old + st[n, h * DH:(h + 1) * DH, :]

        p_out[...] = before[:DH // part].reshape(DH, DH)
        for slot in range(2):
            send_p(slot).start()

        def exchange(d, piece, skip, source):
            partner = lax.rem(me + (groups - d if source else d), groups)
            owner = partner if source else me
            to = pl.ds(pl.multiple_of(piece * PIECE, PIECE), PIECE)
            at = to if source else pl.ds(pl.multiple_of(partner * own + piece * PIECE, PIECE), PIECE)
            cols = pl.ds(pl.multiple_of(owner * width + skip * DH, DH), width - skip * DH)
            return pltpu.make_async_remote_copy(
                src_ref=att.at[at, pl.ds(skip * DH, width - skip * DH)], dst_ref=rcv.at[to, cols],
                send_sem=send_sem.at[d, piece], recv_sem=recv_sem.at[d, piece],
                device_id={"head": partner}, device_id_type=MESH)

        def rows_of(n, half, h):
            hs = slice(h * DH, (h + 1) * DH)
            at = half_of(n, half)
            low = state(n, h).astype(BF16)
            return (acc[at, hs] + dot(q[at, hs], low, ((1,), (0,)))).astype(BF16)

        def finish(d, piece, which):
            n = first_block(d) + piece
            for half in range(2):
                for h in which:
                    att[half_of(n, half), h * DH:(h + 1) * DH] = rows_of(n, half, h)
                for cut in range(cuts):
                    exchange(d, (piece * 2 + half) * cuts + cut, which[0], False).start()

        def finish_sides(piece):
            @pl.loop(0, 2)
            def _(slot):
                finish(1 + 2 * slot, piece, later)

        finish(2, 0, every)
        finish_sides(0)

        @pl.loop(1, per)
        def _(piece):
            keep(first_block(2) + piece, every)
            finish(2, piece, every)
            keep_sides(piece)
            finish_sides(piece)

        @pl.loop(0, per)
        def _(piece):
            n = me * per + piece
            keep(n, every)
            for half in range(2):
                for h in every:
                    cols = pl.ds(pl.multiple_of(me * width + h * DH, DH), DH)
                    rcv[half_of(piece, half), cols] = rows_of(n, half, h)

        for slot in range(2):
            send_q(slot).wait_recv()
            send_p(slot).wait_recv()

        @pl.loop(0, per)
        def _(piece):
            for slot in range(2):
                send_l(slot, piece).wait_recv()
                src = lax.rem(me + groups - 1 - 2 * slot, groups)
                cols = pl.ds(pl.multiple_of(src * width, DH), DH)
                for half in range(2):
                    at = half_of(piece, half)
                    value = dot(q_in[slot, at, :], p_in[slot], ((1,), (0,)))
                    rcv[at, cols] = (l_in[slot, at, :].astype(F32) + value).astype(BF16)

        load_gain.wait()

        @pl.loop(0, pieces)
        def _(i):
            for d, skip in ((1, 1), (3, 1), (2, 0)):
                exchange(d, i, skip, True).wait_recv()

            @pl.loop(0, PIECE // 32)
            def _(j):
                at = pl.ds(pl.multiple_of(i * PIECE + j * 32, 32), 32)
                wide = rcv[at, :].astype(F32)
                mean = jnp.mean(wide * wide, axis=-1, keepdims=True)
                out[at, :] = (wide * lax.rsqrt(mean + 1e-06) * gain[...]).astype(BF16)

        @pl.loop(0, pieces)
        def _(i):
            for d, skip in ((1, 1), (3, 1), (2, 0)):
                exchange(d, i, skip, False).wait_send()

        for slot in range(2):
            send_q(slot).wait_send()
            send_p(slot).wait_send()
            for piece in range(per):
                send_l(slot, piece).wait_send()

        all_of(0).wait_send()
        all_of(1).wait_send()

    return kernel


def solution(mesh):
    seqs, groups = mesh.shape["seq"], mesh.shape["head"]

    def shards(queries, keys, values, norm_gain):
        rows, width = queries.shape
        blocks = rows // BLK
        own = rows // groups
        per = own // BLK
        full = width * groups
        part = width // seqs
        dma = pltpu.SemaphoreType.DMA
        return pl.pallas_call(
            make_kernel(seqs, groups, rows, width),
            out_shape=pltpu.VMEM((own, full), BF16),
            in_specs=[pl.BlockSpec(memory_space=pltpu.HBM)] * 4,
            out_specs=pl.BlockSpec(memory_space=pltpu.VMEM),
            scratch_shapes=[
                pltpu.VMEM((rows, width), BF16),
                pltpu.VMEM((rows, width), BF16),
                pltpu.VMEM((rows, width), BF16),
                pltpu.VMEM((1, full), F32),
                pltpu.VMEM((blocks, width, DH), F32),
                pltpu.VMEM((width, DH), F32),
                pltpu.VMEM((seqs, part, DH), F32),
                pltpu.VMEM((seqs, part, DH), BF16),
                pltpu.VMEM((seqs, part, DH), BF16),
                pltpu.VMEM((rows, width), F32),
                pltpu.VMEM((rows, width), BF16),
                pltpu.VMEM((own, full), BF16),
                pltpu.VMEM((2, own, DH), BF16),
                pltpu.VMEM((2, own, DH), BF16),
                pltpu.VMEM((2, own, DH), BF16),
                pltpu.VMEM((DH, DH), BF16),
                pltpu.VMEM((2, DH, DH), BF16),
                dma((3, blocks)),
                dma,
                dma((2,)),
                dma((2,)),
                dma((groups, own // PIECE)),
                dma((groups, own // PIECE)),
                dma((2, 2)),
                dma((2, 2, per)),
                dma((2, 2)),
            ],
            compiler_params=pltpu.CompilerParams(
                collective_id=0, has_side_effects=True, vmem_limit_bytes=58 << 20),
            name="attention_norm",
        )(queries, keys, values, norm_gain[None, :])

    return jax.shard_map(
        shards,
        mesh=mesh,
        in_specs=(P("seq", "head"), P("seq", "head"), P("seq", "head"), P()),
        out_specs=P(("seq", "head"), None),
        check_vma=False,
    )
```

```python
import jax
import jax.numpy as jnp
from jax import lax
from jax.experimental import pallas as pl
from jax.experimental.pallas import tpu as pltpu
from jax.sharding import PartitionSpec as P

DH = 128
BLK = 512
HALF = BLK // 2
PIECE = 128
MESH = pl.DeviceIdType.MESH
F32 = jnp.float32
BF16 = jnp.bfloat16


def dot(a, b, dims):
    return lax.dot_general(a, b, (dims, ((), ())), preferred_element_type=F32)


def offsets(seqs):
    side = 1
    while side * side * 2 < seqs:
        side += 1
    assert side * side * 2 == seqs

    def hops(step):
        return min(step, side - step)

    steps = [(y, z, c) for y in range(side) for z in range(side) for c in range(2)]
    steps.remove((0, 0, 0))
    return side, sorted(steps, key=lambda s: (-hops(s[0]) - hops(s[1]), s))


def make_kernel(seqs, groups, rows, width):
    assert groups == 4
    heads = width // DH
    blocks = rows // BLK
    own = rows // groups
    part = (heads * DH) // seqs
    per = own // BLK
    pieces = own // PIECE
    cuts = HALF // PIECE
    side, steps = offsets(seqs)
    later = tuple(range(1, heads))
    every = tuple(range(heads))

    def kernel(q_hbm, k_hbm, v_hbm, g_hbm, out, q, k, v, gain, st, tot, got, pre, before, acc, att, rcv,
               q_in, l_out, l_in, p_out, p_in,
               in_sem, gain_sem, scan_send, scan_recv, send_sem, recv_sem, q_sems, l_sems, p_sems):
        me = lax.axis_index("head")
        my = lax.axis_index("seq")

        def block(n):
            return pl.ds(n * BLK if isinstance(n, int) else pl.multiple_of(n * BLK, BLK), BLK)

        def half_of(n, half):
            return pl.ds(pl.multiple_of(n * BLK + half * HALF, HALF), HALF)

        def load(i, n):
            hbm, ref = ((k_hbm, k), (v_hbm, v), (q_hbm, q))[i]
            return pltpu.make_async_copy(hbm.at[block(n)], ref.at[block(n)], in_sem.at[i, n])

        for n in range(blocks):
            load(0, n).start()
            load(1, n).start()
        load_gain = pltpu.make_async_copy(g_hbm, gain, gain_sem)
        load_gain.start()

        my_y, my_z, my_c = my // (2 * side), lax.rem(my // 2, side), lax.rem(my, 2)

        def away(step):
            y = lax.rem(my_y + step[0], side)
            z = lax.rem(my_z + step[1], side)
            return (y * side + z) * 2 + lax.rem(my_c + step[2], 2)

        def first_block(d):
            return lax.rem(me + d, groups) * per

        barrier = pltpu.get_barrier_semaphore()
        for d in range(1, groups):
            pl.semaphore_signal(barrier, inc=1, device_id={"head": lax.rem(me + d, groups)}, device_id_type=MESH)
        for step in steps:
            pl.semaphore_signal(barrier, inc=1, device_id={"seq": away(step)}, device_id_type=MESH)

        def ahead(src, dst, sems, slot, *which):
            return pltpu.make_async_remote_copy(
                src_ref=src, dst_ref=dst, send_sem=sems.at[(0, slot) + which], recv_sem=sems.at[(1, slot) + which],
                device_id={"head": lax.rem(me + 1 + 2 * slot, groups)}, device_id_type=MESH)

        def send_q(slot):
            at = pl.ds(pl.multiple_of(first_block(1 + 2 * slot) * BLK, BLK), own)
            return ahead(q_hbm.at[at, pl.ds(0, DH)], q_in.at[slot], q_sems, slot)

        def send_l(slot, piece):
            return ahead(l_out.at[slot, block(piece)], l_in.at[slot, block(piece)], l_sems, slot, piece)

        def send_p(slot):
            return ahead(p_out, p_in.at[slot], p_sems, slot)

        tot[...] = jnp.zeros_like(tot)

        def gather(start, count):
            for n in range(start, start + count):
                load(0, n).wait()
                load(1, n).wait()
                load(2, n).start()
            for h in range(heads):
                hs = slice(h * DH, (h + 1) * DH)
                run = tot[hs, :]
                for n in range(start, start + count):
                    st[n, hs, :] = run
                    run = run + dot(k[block(n), hs], v[block(n), hs], ((0,), (0,)))
                tot[hs, :] = run

        gather(0, 4)
        gather(4, 2)
        pl.semaphore_wait(barrier, seqs - 1 + groups - 1)
        for slot in range(2):
            send_q(slot).start()
        gather(6, 2)

        def mine(i):
            return pl.ds(pl.multiple_of(i * part, part), part)

        def first(i):
            return pltpu.make_async_remote_copy(
                src_ref=tot.at[mine(i)], dst_ref=got.at[my], send_sem=scan_send.at[0], recv_sem=scan_recv.at[0],
                device_id={"seq": i}, device_id_type=MESH)

        def second(i):
            return pltpu.make_async_remote_copy(
                src_ref=pre.at[i], dst_ref=before.at[my], send_sem=scan_send.at[1], recv_sem=scan_recv.at[1],
                device_id={"seq": i}, device_id_type=MESH)

        def all_of(stage):
            ref = (got, before)[stage].at[pl.ds(0, seqs - 1)]
            return pltpu.make_async_remote_copy(
                src_ref=ref, dst_ref=ref, send_sem=scan_send.at[stage], recv_sem=scan_recv.at[stage],
                device_id={"seq": lax.rem(my + 1, seqs)}, device_id_type=MESH)

        for step in steps:
            first(away(step)).start()

        got[my] = tot[mine(my), :]

        row = lax.broadcasted_iota(jnp.int32, (HALF, HALF), 0)
        col = lax.broadcasted_iota(jnp.int32, (HALF, HALF), 1)
        causal = row >= col

        def local(n, h):
            hs = slice(h * DH, (h + 1) * DH)
            lo, hi = half_of(n, 0), half_of(n, 1)
            k_lo, k_hi, v_lo, v_hi = k[lo, hs], k[hi, hs], v[lo, hs], v[hi, hs]
            q_lo, q_hi = q[lo, hs], q[hi, hs]
            s = jnp.where(causal, dot(q_lo, k_lo, ((1,), (1,))), 0.0).astype(BF16)
            s_l = dot(q_hi, k_lo, ((1,), (1,))).astype(BF16)
            s_h = jnp.where(causal, dot(q_hi, k_hi, ((1,), (1,))), 0.0).astype(BF16)
            return (dot(s, v_lo, ((1,), (0,))),
                    dot(s_l, v_lo, ((1,), (0,))) + dot(s_h, v_hi, ((1,), (0,))))

        for n in range(blocks):
            load(2, n).wait()

        @pl.loop(0, per)
        def _(piece):
            for slot in range(2):
                n = first_block(1 + 2 * slot) + piece
                low = st[n, :DH, :].astype(BF16)
                for half, value in enumerate(local(n, 0)):
                    value = value + dot(q[half_of(n, half), :DH], low, ((1,), (0,)))
                    l_out[slot, half_of(piece, half), :] = value.astype(BF16)
                send_l(slot, piece).start()

        def keep(n, which):
            for h in which:
                hs = slice(h * DH, (h + 1) * DH)
                acc[half_of(n, 0), hs], acc[half_of(n, 1), hs] = local(n, h)

        def keep_sides(piece):
            @pl.loop(0, 2)
            def _(slot):
                keep(first_block(1 + 2 * slot) + piece, later)

        all_of(0).wait_recv()
        run = jnp.zeros((part, DH), F32)
        for i in range(seqs):
            pre[i] = run.astype(BF16)
            run = run + got[i]

        for step in steps:
            second(away(step)).start()

        before[my] = pre[my]

        keep_sides(0)
        keep(first_block(2), every)

        all_of(1).wait_recv()

        def state(n, h):
            some = slice(h * DH // part, (h + 1) * DH // part)
            old = before[some].reshape(DH, DH).astype(F32)
            return old + st[n, h * DH:(h + 1) * DH, :]

        p_out[...] = before[:DH // part].reshape(DH, DH)
        for slot in range(2):
            send_p(slot).start()

        def exchange(d, piece, skip, source):
            partner = lax.rem(me + (groups - d if source else d), groups)
            owner = partner if source else me
            to = pl.ds(pl.multiple_of(piece * PIECE, PIECE), PIECE)
            at = to if source else pl.ds(pl.multiple_of(partner * own + piece * PIECE, PIECE), PIECE)
            cols = pl.ds(pl.multiple_of(owner * width + skip * DH, DH), width - skip * DH)
            return pltpu.make_async_remote_copy(
                src_ref=att.at[at, pl.ds(skip * DH, width - skip * DH)], dst_ref=rcv.at[to, cols],
                send_sem=send_sem.at[d, piece], recv_sem=recv_sem.at[d, piece],
                device_id={"head": partner}, device_id_type=MESH)

        def rows_of(n, half, h):
            hs = slice(h * DH, (h + 1) * DH)
            at = half_of(n, half)
            low = state(n, h).astype(BF16)
            return (acc[at, hs] + dot(q[at, hs], low, ((1,), (0,)))).astype(BF16)

        def finish(d, piece, which):
            n = first_block(d) + piece
            for half in range(2):
                for h in which:
                    att[half_of(n, half), h * DH:(h + 1) * DH] = rows_of(n, half, h)
                for cut in range(cuts):
                    exchange(d, (piece * 2 + half) * cuts + cut, which[0], False).start()

        def finish_sides(piece):
            @pl.loop(0, 2)
            def _(slot):
                finish(1 + 2 * slot, piece, later)

        finish(2, 0, every)
        finish_sides(0)

        @pl.loop(1, per)
        def _(piece):
            keep(first_block(2) + piece, every)
            finish(2, piece, every)
            keep_sides(piece)
            finish_sides(piece)

        @pl.loop(0, per)
        def _(piece):
            n = me * per + piece
            keep(n, every)
            for half in range(2):
                for h in every:
                    cols = pl.ds(pl.multiple_of(me * width + h * DH, DH), DH)
                    rcv[half_of(piece, half), cols] = rows_of(n, half, h)

        for slot in range(2):
            send_q(slot).wait_recv()
            send_p(slot).wait_recv()

        @pl.loop(0, per)
        def _(piece):
            for slot in range(2):
                send_l(slot, piece).wait_recv()
                src = lax.rem(me + groups - 1 - 2 * slot, groups)
                cols = pl.ds(pl.multiple_of(src * width, DH), DH)
                for half in range(2):
                    at = half_of(piece, half)
                    value = dot(q_in[slot, at, :], p_in[slot], ((1,), (0,)))
                    rcv[at, cols] = (l_in[slot, at, :].astype(F32) + value).astype(BF16)

        for slot in range(2):
            send_q(slot).wait_send()
            send_p(slot).wait_send()
            for piece in range(per):
                send_l(slot, piece).wait_send()

        all_of(0).wait_send()
        all_of(1).wait_send()

        load_gain.wait()

        @pl.loop(0, pieces)
        def _(i):
            @pl.when(i > 0)
            def _():
                for d, skip in ((1, 1), (3, 1), (2, 0)):
                    exchange(d, i - 1, skip, False).wait_send()

            for d, skip in ((1, 1), (3, 1), (2, 0)):
                exchange(d, i, skip, True).wait_recv()

            @pl.loop(0, PIECE // 32, unroll=PIECE // 32)
            def _(j):
                at = pl.ds(pl.multiple_of(i * PIECE + j * 32, 32), 32)
                wide = rcv[at, :].astype(F32)
                mean = jnp.mean(wide * wide, axis=-1, keepdims=True)
                out[at, :] = (wide * lax.rsqrt(mean + 1e-06) * gain[...]).astype(BF16)

        for d, skip in ((1, 1), (3, 1), (2, 0)):
            exchange(d, pieces - 1, skip, False).wait_send()

    return kernel


def solution(mesh):
    seqs, groups = mesh.shape["seq"], mesh.shape["head"]

    def shards(queries, keys, values, norm_gain):
        rows, width = queries.shape
        blocks = rows // BLK
        own = rows // groups
        per = own // BLK
        full = width * groups
        part = width // seqs
        dma = pltpu.SemaphoreType.DMA
        return pl.pallas_call(
            make_kernel(seqs, groups, rows, width),
            out_shape=pltpu.VMEM((own, full), BF16),
            in_specs=[pl.BlockSpec(memory_space=pltpu.HBM)] * 4,
            out_specs=pl.BlockSpec(memory_space=pltpu.VMEM),
            scratch_shapes=[
                pltpu.VMEM((rows, width), BF16),
                pltpu.VMEM((rows, width), BF16),
                pltpu.VMEM((rows, width), BF16),
                pltpu.VMEM((1, full), F32),
                pltpu.VMEM((blocks, width, DH), F32),
                pltpu.VMEM((width, DH), F32),
                pltpu.VMEM((seqs, part, DH), F32),
                pltpu.VMEM((seqs, part, DH), BF16),
                pltpu.VMEM((seqs, part, DH), BF16),
                pltpu.VMEM((rows, width), F32),
                pltpu.VMEM((rows, width), BF16),
                pltpu.VMEM((own, full), BF16),
                pltpu.VMEM((2, own, DH), BF16),
                pltpu.VMEM((2, own, DH), BF16),
                pltpu.VMEM((2, own, DH), BF16),
                pltpu.VMEM((DH, DH), BF16),
                pltpu.VMEM((2, DH, DH), BF16),
                dma((3, blocks)),
                dma,
                dma((2,)),
                dma((2,)),
                dma((groups, own // PIECE)),
                dma((groups, own // PIECE)),
                dma((2, 2)),
                dma((2, 2, per)),
                dma((2, 2)),
            ],
            compiler_params=pltpu.CompilerParams(
                collective_id=0, has_side_effects=True, vmem_limit_bytes=58 << 20),
            name="attention_norm",
        )(queries, keys, values, norm_gain[None, :])

    return jax.shard_map(
        shards,
        mesh=mesh,
        in_specs=(P("seq", "head"), P("seq", "head"), P("seq", "head"), P()),
        out_specs=P(("seq", "head"), None),
        check_vma=False,
    )
```

```python
import jax
import jax.numpy as jnp
from jax import lax
from jax.experimental import pallas as pl
from jax.experimental.pallas import tpu as pltpu
from jax.sharding import PartitionSpec as P

DH = 128
BLK = 512
HALF = BLK // 2
PIECE = 128
MESH = pl.DeviceIdType.MESH
F32 = jnp.float32
BF16 = jnp.bfloat16


def dot(a, b, dims):
    return lax.dot_general(a, b, (dims, ((), ())), preferred_element_type=F32)


def offsets(seqs):
    side = 1
    while side * side * 2 < seqs:
        side += 1
    assert side * side * 2 == seqs

    def hops(step):
        return min(step, side - step)

    steps = [(y, z, c) for y in range(side) for z in range(side) for c in range(2)]
    steps.remove((0, 0, 0))
    return side, sorted(steps, key=lambda s: (-hops(s[0]) - hops(s[1]), s))


def make_kernel(seqs, groups, rows, width):
    assert groups == 4
    heads = width // DH
    blocks = rows // BLK
    own = rows // groups
    part = (heads * DH) // seqs
    per = own // BLK
    pieces = own // PIECE
    cuts = HALF // PIECE
    side, steps = offsets(seqs)
    later = tuple(range(1, heads))
    every = tuple(range(heads))

    def kernel(q_hbm, k_hbm, v_hbm, g_hbm, out, q, k, v, gain, st, tot, got, pre, before, acc, att, rcv,
               q_in, l_out, l_in, p_out, p_in,
               in_sem, gain_sem, scan_send, scan_recv, send_sem, recv_sem, q_sems, l_sems, p_sems):
        me = lax.axis_index("head")
        my = lax.axis_index("seq")

        def block(n):
            return pl.ds(n * BLK if isinstance(n, int) else pl.multiple_of(n * BLK, BLK), BLK)

        def half_of(n, half):
            return pl.ds(pl.multiple_of(n * BLK + half * HALF, HALF), HALF)

        def load(i, n):
            hbm, ref = ((k_hbm, k), (v_hbm, v), (q_hbm, q))[i]
            return pltpu.make_async_copy(hbm.at[block(n)], ref.at[block(n)], in_sem.at[i, n])

        for n in range(blocks):
            load(0, n).start()
            load(1, n).start()
        load_gain = pltpu.make_async_copy(g_hbm, gain, gain_sem)
        load_gain.start()

        my_y, my_z, my_c = my // (2 * side), lax.rem(my // 2, side), lax.rem(my, 2)

        def away(step):
            y = lax.rem(my_y + step[0], side)
            z = lax.rem(my_z + step[1], side)
            return (y * side + z) * 2 + lax.rem(my_c + step[2], 2)

        def first_block(d):
            return lax.rem(me + d, groups) * per

        barrier = pltpu.get_barrier_semaphore()
        for d in range(1, groups):
            pl.semaphore_signal(barrier, inc=1, device_id={"head": lax.rem(me + d, groups)}, device_id_type=MESH)
        for step in steps:
            pl.semaphore_signal(barrier, inc=1, device_id={"seq": away(step)}, device_id_type=MESH)

        def ahead(src, dst, sems, slot, *which):
            return pltpu.make_async_remote_copy(
                src_ref=src, dst_ref=dst, send_sem=sems.at[(0, slot) + which], recv_sem=sems.at[(1, slot) + which],
                device_id={"head": lax.rem(me + 1 + 2 * slot, groups)}, device_id_type=MESH)

        def send_q(slot):
            at = pl.ds(pl.multiple_of(first_block(1 + 2 * slot) * BLK, BLK), own)
            return ahead(q_hbm.at[at, pl.ds(0, DH)], q_in.at[slot], q_sems, slot)

        def send_l(slot, piece):
            return ahead(l_out.at[slot, block(piece)], l_in.at[slot, block(piece)], l_sems, slot, piece)

        def send_p(slot):
            return ahead(p_out, p_in.at[slot], p_sems, slot)

        tot[...] = jnp.zeros_like(tot)

        def gather(start, count):
            for n in range(start, start + count):
                load(0, n).wait()
                load(1, n).wait()
                load(2, n).start()
            for h in range(heads):
                hs = slice(h * DH, (h + 1) * DH)
                run = tot[hs, :]
                for n in range(start, start + count):
                    st[n, hs, :] = run
                    run = run + dot(k[block(n), hs], v[block(n), hs], ((0,), (0,)))
                tot[hs, :] = run

        gather(0, 2)
        gather(2, 2)
        gather(4, 2)
        pl.semaphore_wait(barrier, seqs - 1 + groups - 1)
        for slot in range(2):
            send_q(slot).start()
        gather(6, 2)

        def mine(i):
            return pl.ds(pl.multiple_of(i * part, part), part)

        def first(i):
            return pltpu.make_async_remote_copy(
                src_ref=tot.at[mine(i)], dst_ref=got.at[my], send_sem=scan_send.at[0], recv_sem=scan_recv.at[0],
                device_id={"seq": i}, device_id_type=MESH)

        def second(i):
            return pltpu.make_async_remote_copy(
                src_ref=pre.at[i], dst_ref=before.at[my], send_sem=scan_send.at[1], recv_sem=scan_recv.at[1],
                device_id={"seq": i}, device_id_type=MESH)

        def all_of(stage):
            ref = (got, before)[stage].at[pl.ds(0, seqs - 1)]
            return pltpu.make_async_remote_copy(
                src_ref=ref, dst_ref=ref, send_sem=scan_send.at[stage], recv_sem=scan_recv.at[stage],
                device_id={"seq": lax.rem(my + 1, seqs)}, device_id_type=MESH)

        for step in steps:
            first(away(step)).start()

        got[my] = tot[mine(my), :]

        row = lax.broadcasted_iota(jnp.int32, (HALF, HALF), 0)
        col = lax.broadcasted_iota(jnp.int32, (HALF, HALF), 1)
        causal = row >= col

        def local(n, h):
            hs = slice(h * DH, (h + 1) * DH)
            lo, hi = half_of(n, 0), half_of(n, 1)
            k_lo, k_hi, v_lo, v_hi = k[lo, hs], k[hi, hs], v[lo, hs], v[hi, hs]
            q_lo, q_hi = q[lo, hs], q[hi, hs]
            s = jnp.where(causal, dot(q_lo, k_lo, ((1,), (1,))), 0.0).astype(BF16)
            s_l = dot(q_hi, k_lo, ((1,), (1,))).astype(BF16)
            s_h = jnp.where(causal, dot(q_hi, k_hi, ((1,), (1,))), 0.0).astype(BF16)
            return (dot(s, v_lo, ((1,), (0,))),
                    dot(s_l, v_lo, ((1,), (0,))) + dot(s_h, v_hi, ((1,), (0,))))

        for n in range(blocks):
            load(2, n).wait()

        @pl.loop(0, per)
        def _(piece):
            for slot in range(2):
                n = first_block(1 + 2 * slot) + piece
                low = st[n, :DH, :].astype(BF16)
                for half, value in enumerate(local(n, 0)):
                    value = value + dot(q[half_of(n, half), :DH], low, ((1,), (0,)))
                    l_out[slot, half_of(piece, half), :] = value.astype(BF16)
                send_l(slot, piece).start()

        def keep(n, which):
            for h in which:
                hs = slice(h * DH, (h + 1) * DH)
                acc[half_of(n, 0), hs], acc[half_of(n, 1), hs] = local(n, h)

        def keep_sides(piece):
            @pl.loop(0, 2)
            def _(slot):
                keep(first_block(1 + 2 * slot) + piece, later)

        all_of(0).wait_recv()
        run = jnp.zeros((part, DH), F32)
        for i in range(seqs):
            pre[i] = run.astype(BF16)
            run = run + got[i]

        for step in steps:
            second(away(step)).start()

        before[my] = pre[my]

        keep_sides(0)
        keep(first_block(2), every)

        all_of(1).wait_recv()

        def state(n, h):
            some = slice(h * DH // part, (h + 1) * DH // part)
            old = before[some].reshape(DH, DH).astype(F32)
            return old + st[n, h * DH:(h + 1) * DH, :]

        p_out[...] = before[:DH // part].reshape(DH, DH)
        for slot in range(2):
            send_p(slot).start()

        def exchange(d, piece, skip, source):
            partner = lax.rem(me + (groups - d if source else d), groups)
            owner = partner if source else me
            to = pl.ds(pl.multiple_of(piece * PIECE, PIECE), PIECE)
            at = to if source else pl.ds(pl.multiple_of(partner * own + piece * PIECE, PIECE), PIECE)
            cols = pl.ds(pl.multiple_of(owner * width + skip * DH, DH), width - skip * DH)
            return pltpu.make_async_remote_copy(
                src_ref=att.at[at, pl.ds(skip * DH, width - skip * DH)], dst_ref=rcv.at[to, cols],
                send_sem=send_sem.at[d, piece], recv_sem=recv_sem.at[d, piece],
                device_id={"head": partner}, device_id_type=MESH)

        def rows_of(n, half, h):
            hs = slice(h * DH, (h + 1) * DH)
            at = half_of(n, half)
            low = state(n, h).astype(BF16)
            return (acc[at, hs] + dot(q[at, hs], low, ((1,), (0,)))).astype(BF16)

        def finish(d, piece, which):
            n = first_block(d) + piece
            for half in range(2):
                for h in which:
                    att[half_of(n, half), h * DH:(h + 1) * DH] = rows_of(n, half, h)
                for cut in range(cuts):
                    exchange(d, (piece * 2 + half) * cuts + cut, which[0], False).start()

        def finish_sides(piece):
            @pl.loop(0, 2)
            def _(slot):
                finish(1 + 2 * slot, piece, later)

        finish(2, 0, every)
        finish_sides(0)

        @pl.loop(1, per)
        def _(piece):
            keep(first_block(2) + piece, every)
            finish(2, piece, every)
            keep_sides(piece)
            finish_sides(piece)

        @pl.loop(0, per)
        def _(piece):
            n = me * per + piece
            keep(n, every)
            for half in range(2):
                for h in every:
                    cols = pl.ds(pl.multiple_of(me * width + h * DH, DH), DH)
                    rcv[half_of(piece, half), cols] = rows_of(n, half, h)

        for slot in range(2):
            send_q(slot).wait_recv()
            send_p(slot).wait_recv()

        @pl.loop(0, per)
        def _(piece):
            for slot in range(2):
                send_l(slot, piece).wait_recv()
                src = lax.rem(me + groups - 1 - 2 * slot, groups)
                cols = pl.ds(pl.multiple_of(src * width, DH), DH)
                for half in range(2):
                    at = half_of(piece, half)
                    value = dot(q_in[slot, at, :], p_in[slot], ((1,), (0,)))
                    rcv[at, cols] = (l_in[slot, at, :].astype(F32) + value).astype(BF16)

        for slot in range(2):
            send_q(slot).wait_send()
            send_p(slot).wait_send()
            for piece in range(per):
                send_l(slot, piece).wait_send()

        all_of(0).wait_send()
        all_of(1).wait_send()

        load_gain.wait()

        @pl.loop(0, pieces)
        def _(i):
            @pl.when(i > 0)
            def _():
                for d, skip in ((1, 1), (3, 1), (2, 0)):
                    exchange(d, i - 1, skip, False).wait_send()

            for d, skip in ((1, 1), (3, 1), (2, 0)):
                exchange(d, i, skip, True).wait_recv()

            @pl.loop(0, PIECE // 32, unroll=PIECE // 32)
            def _(j):
                at = pl.ds(pl.multiple_of(i * PIECE + j * 32, 32), 32)
                wide = rcv[at, :].astype(F32)
                mean = jnp.mean(wide * wide, axis=-1, keepdims=True)
                out[at, :] = (wide * lax.rsqrt(mean + 1e-06) * gain[...]).astype(BF16)

        for d, skip in ((1, 1), (3, 1), (2, 0)):
            exchange(d, pieces - 1, skip, False).wait_send()

    return kernel


def solution(mesh):
    seqs, groups = mesh.shape["seq"], mesh.shape["head"]

    def shards(queries, keys, values, norm_gain):
        rows, width = queries.shape
        blocks = rows // BLK
        own = rows // groups
        per = own // BLK
        full = width * groups
        part = width // seqs
        dma = pltpu.SemaphoreType.DMA
        return pl.pallas_call(
            make_kernel(seqs, groups, rows, width),
            out_shape=pltpu.VMEM((own, full), BF16),
            in_specs=[pl.BlockSpec(memory_space=pltpu.HBM)] * 4,
            out_specs=pl.BlockSpec(memory_space=pltpu.VMEM),
            scratch_shapes=[
                pltpu.VMEM((rows, width), BF16),
                pltpu.VMEM((rows, width), BF16),
                pltpu.VMEM((rows, width), BF16),
                pltpu.VMEM((1, full), F32),
                pltpu.VMEM((blocks, width, DH), F32),
                pltpu.VMEM((width, DH), F32),
                pltpu.VMEM((seqs, part, DH), F32),
                pltpu.VMEM((seqs, part, DH), BF16),
                pltpu.VMEM((seqs, part, DH), BF16),
                pltpu.VMEM((rows, width), F32),
                pltpu.VMEM((rows, width), BF16),
                pltpu.VMEM((own, full), BF16),
                pltpu.VMEM((2, own, DH), BF16),
                pltpu.VMEM((2, own, DH), BF16),
                pltpu.VMEM((2, own, DH), BF16),
                pltpu.VMEM((DH, DH), BF16),
                pltpu.VMEM((2, DH, DH), BF16),
                dma((3, blocks)),
                dma,
                dma((2,)),
                dma((2,)),
                dma((groups, own // PIECE)),
                dma((groups, own // PIECE)),
                dma((2, 2)),
                dma((2, 2, per)),
                dma((2, 2)),
            ],
            compiler_params=pltpu.CompilerParams(
                collective_id=0, has_side_effects=True, vmem_limit_bytes=58 << 20),
            name="attention_norm",
        )(queries, keys, values, norm_gain[None, :])

    return jax.shard_map(
        shards,
        mesh=mesh,
        in_specs=(P("seq", "head"), P("seq", "head"), P("seq", "head"), P()),
        out_specs=P(("seq", "head"), None),
        check_vma=False,
    )
```
